256 devices in a mesh: layer: 16 (over z, core), dp: 16 (over x, y).
Axes of the slice: x: 4, y: 4, z: 8, core: 2. Of those that a mesh axis runs over, the one named last changes fastest.
Arguments:
- starts: float32 [16, 16, 32, 32, 128], P('layer', 'dp'), may hold values from -6 to 6
- weights: bfloat16 [64, 9, 128, 128], P('layer'), may hold values from -0.1875 to 0.1875
- biases: bfloat16 [64, 128], P('layer'), may hold values from -3 to 3
- adj_ends: float32 [16, 16, 32, 32, 128], P('layer', 'dp'), may hold values from -6 to 6
Outputs:
- block_ends: float32 [16, 16, 32, 32, 128], P('layer', 'dp')
- adjoint_starts: float32 [16, 16, 32, 32, 128], P('layer', 'dp')
- weight_grad: float32 [64, 9, 128, 128], P('layer')
- bias_grad: float32 [64, 128], P('layer')
The draws below stay inside these ranges and needn't reach their ends.
All inputs are finite; a program needn't handle non-finite values.
Results may differ from the reference program's by a relative error of at most 0.039.
Values may be sent and summed in bfloat16 or wider, within the bound.
No kernel may reach another device: no remote copies, remote signals or barrier semaphores. Data moves between devices by JAX's collectives and lax.ppermute only.
A program may use at most 64 MiB of HBM per device.

```python
import math
import jax
import jax.numpy as jnp
from jax import lax

C = 128
MAP = 32
LAYERS = 64
IMAGES = 16
N_LAYER = 16


def level_of(stream_key, dims, cuts, smallest, largest):
    loudness = 1.0
    for axis_at, shards_of in cuts:
        steps = jax.random.uniform(jax.random.fold_in(jax.random.fold_in(stream_key, 6), axis_at), (shards_of,), jnp.float32, smallest / len(cuts), largest / len(cuts))
        loudness = loudness * jnp.repeat(jnp.exp(steps), dims[axis_at] // shards_of).reshape((-1,) + (1,) * (len(dims) - 1 - axis_at))
    return loudness


def noise(stream_key, shape, spread, reach, cuts=(), dtype=jnp.bfloat16):
    loudness = level_of(stream_key, shape, cuts, -0.22, 0.18) if cuts else 1.0
    array = jax.random.normal(stream_key, shape, jnp.float32) * spread * loudness
    return jnp.minimum(jnp.maximum(array, -reach), reach).astype(dtype)


def setup_inputs(seed: int = 0) -> dict:
    streams_of = jax.random.split(jax.random.key(seed), 5)
    starts = noise(streams_of[0], (N_LAYER, IMAGES, MAP, MAP, C), 1.0, 6.0, ((0, 16), (1, 16)), jnp.float32)
    weights = noise(streams_of[1], (LAYERS, 9, C, C), (9 * C) ** -0.5, 0.1875, ((0, 16),))
    biases = noise(streams_of[2], (LAYERS, C), 0.5, 3.0, ((0, 16),))
    adj_ends = noise(streams_of[3], (N_LAYER, IMAGES, MAP, MAP, C), 1.0, 6.0, ((0, 16), (1, 16)), jnp.float32)
    return {"starts": starts, "weights": weights, "biases": biases, "adj_ends": adj_ends}


step_size = 0.25

def convolve(rounded, kernel):
    count, map_side, _, channels = rounded.shape
    padded = jnp.pad(rounded, ((0, 0), (1, 1), (1, 1), (0, 0)))
    running = jnp.zeros((count * map_side * map_side, kernel.shape[2]), jnp.float32)
    for tap_index in range(9):
        row_off = tap_index // 3
        col_off = tap_index % 3
        view = padded[:, row_off:row_off + map_side, col_off:col_off + map_side, :].reshape(count * map_side * map_side, channels)
        running = running + jnp.dot(view, kernel[tap_index], preferred_element_type=jnp.float32)
    return running.reshape(count, map_side, map_side, kernel.shape[2])

def transposed(signal, kernel):
    count, map_side, _, channels = signal.shape
    padded = jnp.pad(signal, ((0, 0), (1, 1), (1, 1), (0, 0)))
    running = jnp.zeros((count * map_side * map_side, kernel.shape[1]), jnp.float32)
    for tap_index in range(9):
        row_off = 2 - tap_index // 3
        col_off = 2 - tap_index % 3
        view = padded[:, row_off:row_off + map_side, col_off:col_off + map_side, :].reshape(count * map_side * map_side, channels)
        running = running + lax.dot_general(view, kernel[tap_index], (((1,), (1,)), ((), ())), preferred_element_type=jnp.float32)
    return running.reshape(count, map_side, map_side, kernel.shape[1])

def correlate(rounded, signal):
    count, map_side, _, channels = rounded.shape
    padded = jnp.pad(rounded, ((0, 0), (1, 1), (1, 1), (0, 0)))
    flat_signal = signal.reshape(count * map_side * map_side, signal.shape[3])
    pieces = []
    for tap_index in range(9):
        row_off = tap_index // 3
        col_off = tap_index % 3
        view = padded[:, row_off:row_off + map_side, col_off:col_off + map_side, :].reshape(count * map_side * map_side, channels)
        pieces.append(lax.dot_general(view, flat_signal, (((0,), (0,)), ((), ())), preferred_element_type=jnp.float32))
    return jnp.stack(pieces)

def activation_of(current_state, kernel, bias_row):
    preact = convolve(current_state.astype(jnp.bfloat16), kernel) + bias_row.astype(jnp.float32)
    return jnp.tanh(preact)

def reference(starts, weights, biases, adj_ends):
    blocks = starts.shape[0]
    block_depth = weights.shape[0] // blocks
    coarse_step = block_depth * step_size
    map_side = starts.shape[2]
    grad_scale = 1.0 / (map_side * math.sqrt(starts.shape[1]))
    relaxed = []
    for block_pos in range(blocks):
        current_state = starts[block_pos]
        for inner_pos in range(block_depth):
            layer_pos = block_pos * block_depth + inner_pos
            current_state = current_state + step_size * activation_of(current_state, weights[layer_pos], biases[layer_pos])
        relaxed.append(current_state)

    def coarse_apply(current_state, block_pos):
        layer_pos = block_pos * block_depth
        return current_state + coarse_step * activation_of(current_state, weights[layer_pos], biases[layer_pos])
    coarse_list = [starts[0]]
    for block_pos in range(blocks - 1):
        coarse_list.append(relaxed[block_pos] - coarse_apply(starts[block_pos], block_pos) + coarse_apply(coarse_list[block_pos], block_pos))
    fine_states = []
    activations = []
    ends_list = []
    for block_pos in range(blocks):
        current_state = coarse_list[block_pos]
        for inner_pos in range(block_depth):
            layer_pos = block_pos * block_depth + inner_pos
            fine_states.append(current_state)
            activation = activation_of(current_state, weights[layer_pos], biases[layer_pos])
            activations.append(activation)
            current_state = current_state + step_size * activation
        ends_list.append(current_state)
    backed = []
    for block_pos in range(blocks):
        adjoint = adj_ends[block_pos]
        for inner_pos in reversed(range(block_depth)):
            layer_pos = block_pos * block_depth + inner_pos
            activation = activations[layer_pos]
            signal = ((1.0 - activation * activation) * adjoint).astype(jnp.bfloat16)
            adjoint = adjoint + step_size * transposed(signal, weights[layer_pos])
        backed.append(adjoint)
    exits = [None] * blocks
    exits[blocks - 1] = adj_ends[blocks - 1]
    for block_pos in range(blocks - 1, 0, -1):
        layer_pos = block_pos * block_depth
        activation = activations[layer_pos]
        difference = exits[block_pos] - adj_ends[block_pos]
        signal = ((1.0 - activation * activation) * difference).astype(jnp.bfloat16)
        exits[block_pos - 1] = backed[block_pos] + (difference + coarse_step * transposed(signal, weights[layer_pos]))
    starts_list = []
    kernel_grads = [None] * weights.shape[0]
    bias_grads = [None] * weights.shape[0]
    for block_pos in range(blocks):
        adjoint = exits[block_pos]
        for inner_pos in reversed(range(block_depth)):
            layer_pos = block_pos * block_depth + inner_pos
            activation = activations[layer_pos]
            signal = ((1.0 - activation * activation) * adjoint).astype(jnp.bfloat16)
            kernel_grads[layer_pos] = correlate(fine_states[layer_pos].astype(jnp.bfloat16), signal) * grad_scale
            bias_grads[layer_pos] = lax.optimization_barrier(jnp.sum(signal.astype(jnp.float32), axis=(0, 1, 2))) * grad_scale
            adjoint = adjoint + step_size * transposed(signal, weights[layer_pos])
        starts_list.append(adjoint)
    return (jnp.stack(ends_list), jnp.stack(starts_list), jnp.stack(kernel_grads), jnp.stack(bias_grads))
```

```python
import functools
import math

import jax
import jax.numpy as jnp
from jax import lax
from jax.experimental import pallas as pl
from jax.experimental.pallas import tpu as pltpu
from jax.sharding import PartitionSpec as P

F32 = jnp.float32
BF16 = jnp.bfloat16
step_size = 0.25
SIDE = 32
PIX = SIDE * SIDE
CH = 128
DEPTH = 4
TAPS = 9
ROWS = TAPS * CH
COARSE = DEPTH * step_size
SEG = 6
SPOT = 3
LOWS = (2, 8)
HEADS = tuple(low + SPOT for low in LOWS)
FIRST, LAST = 1, 14
END = 15
MSG = PIX + ROWS + 16
PEERS = 16
PIECE = DEPTH * ROWS // PEERS
MAIN = 512

VMEM = pl.BlockSpec(memory_space=pltpu.VMEM)
SMEM = pl.BlockSpec(memory_space=pltpu.SMEM)


def shape(rows, dtype):
    return jax.ShapeDtypeStruct(rows, dtype)


IMAGE = (PIX, CH)
PADDED = pltpu.VMEM((PIX + 16, CH), F32)
COLUMNS = pltpu.VMEM((PIX + 2 * SIDE, 3 * CH), BF16)


def call(kernel, outs, ins, scratch):
    return pl.pallas_call(
        kernel,
        out_shape=outs,
        in_specs=ins,
        out_specs=jax.tree.map(lambda _: VMEM, outs),
        scratch_shapes=scratch,
    )


def clear(padded, columns):
    padded[0:8, :] = jnp.zeros((8, CH), F32)
    padded[PIX + 8 : PIX + 16, :] = jnp.zeros((8, CH), F32)
    columns[0:SIDE, :] = jnp.zeros((SIDE, 3 * CH), BF16)
    columns[PIX + SIDE : PIX + 2 * SIDE, :] = jnp.zeros((SIDE, 3 * CH), BF16)


def spread(padded, columns):
    chunk = 256
    place = lax.broadcasted_iota(jnp.int32, (chunk, CH), 0) % SIDE
    has_left, has_right = place != 0, place != SIDE - 1
    for row in range(0, PIX, chunk):
        to = slice(SIDE + row, SIDE + row + chunk)
        left = padded[7 + row : 7 + row + chunk, :]
        right = padded[9 + row : 9 + row + chunk, :]
        columns[to, 0:CH] = jnp.where(has_left, left, 0.0).astype(BF16)
        columns[to, CH : 2 * CH] = padded[8 + row : 8 + row + chunk, :].astype(BF16)
        columns[to, 2 * CH : 3 * CH] = jnp.where(has_right, right, 0.0).astype(BF16)


def windows(columns, row, rows):
    return jnp.concatenate(
        [columns[row + dy * SIDE : row + dy * SIDE + rows, :] for dy in range(3)], axis=1
    )


def forward_dot(columns, row, kernel):
    return jnp.dot(windows(columns, row, MAIN), kernel, preferred_element_type=F32)


def backward_dot(columns, row, kernel):
    return lax.dot_general(
        windows(columns, row, MAIN), kernel, (((1,), (1,)), ((), ())), preferred_element_type=F32
    )


def turned(taps):
    return jnp.concatenate([taps[(8 - t) * CH : (9 - t) * CH, :] for t in range(TAPS)], axis=1)


def relax_kernel(me, start, kernels, biases, short, message, state, columns, first):
    clear(state, columns)
    state[8 : PIX + 8, :] = start[...]

    def layer(n, _):
        spread(state, columns)
        kernel = kernels[n]
        bias = biases[n]
        for row in range(0, PIX, MAIN):
            at = slice(8 + row, 8 + row + MAIN)
            act = jnp.tanh(forward_dot(columns, row, kernel) + bias)
            state[at, :] = state[at, :] + step_size * act

            @pl.when(n == 0)
            def _():
                first[row : row + MAIN, :] = act

        return 0

    lax.fori_loop(0, DEPTH, layer, 0)
    message[PIX : PIX + ROWS, :] = kernels[0]
    message[PIX + ROWS :, :] = jnp.broadcast_to(biases[0], (16, CH)).astype(BF16)
    keep = jnp.where(me[0] == 0, 0.0, 1.0)
    for row in range(0, PIX, MAIN):
        rows = slice(row, row + MAIN)
        guess = start[rows, :] + COARSE * first[rows, :]
        offset = (state[8 + row : 8 + row + MAIN, :] - keep * guess).astype(BF16)
        short[rows, :] = offset
        message[rows, :] = offset


def forward_kernel(count, head, past, carried, me, entry, *refs):
    messages = refs[:count]
    held, refs = refs[count : count + carried], refs[count + carried :]
    leave, slopes, marks = refs[0], refs[1], refs[2 : 2 + count]
    state, columns = refs[-2:]

    if held:

        @pl.when(me[0] == past)
        def _():
            for old, new in zip(held, (slopes,) + tuple(marks)):
                new[...] = old[...]

    @pl.when(me[0] == head)
    def _():
        clear(state, columns)
        state[8 : PIX + 8, :] = entry[...].astype(F32)
        for k in range(count):
            if count > 1:
                marks[k][...] = state[8 : PIX + 8, :].astype(BF16)
            spread(state, columns)
            kernel = messages[k][PIX : PIX + ROWS, :]
            bias = messages[k][PIX + ROWS : PIX + ROWS + 1, :].astype(F32)
            for row in range(0, PIX, MAIN):
                at = slice(8 + row, 8 + row + MAIN)
                rows = slice(row, row + MAIN)
                act = jnp.tanh(forward_dot(columns, row, kernel) + bias)
                slopes[k, rows, :] = (1.0 - act * act).astype(BF16)
                state[at, :] = messages[k][rows, :].astype(F32) + (state[at, :] + COARSE * act)
        leave[...] = state[8 : PIX + 8, :].astype(BF16)


def forward_chain(head, past, me, entry, messages, held):
    count = len(messages)
    marks = count if count > 1 else 1
    outs = [shape(IMAGE, BF16), shape((count,) + IMAGE, BF16)]
    outs += [shape(IMAGE if count > 1 else (16, CH), BF16)] * marks
    out = call(
        functools.partial(forward_kernel, count, head, past, len(held)),
        outs,
        [SMEM] + [VMEM] * (1 + count + len(held)),
        [PADDED, COLUMNS],
    )(me, entry, *messages, *held)
    return out[0], out[1:]


def backward_kernel(count, head, past, carried, me, entry, slopes, *refs):
    terms = refs[:count]
    messages = refs[count : 2 * count]
    held, refs = refs[2 * count : 2 * count + carried], refs[2 * count + carried :]
    leave, marks = refs[0], refs[1 : 1 + count]
    signal, columns, change = refs[1 + count :]

    if held:

        @pl.when(me[0] == past)
        def _():
            for old, new in zip(held, marks):
                new[...] = old[...]

    @pl.when(me[0] == head)
    def _():
        clear(signal, columns)
        change[...] = entry[...].astype(F32)
        for k in reversed(range(count)):
            if count > 1:
                marks[k][...] = change[...].astype(BF16)
            signal[8 : PIX + 8, :] = slopes[k].astype(F32) * change[...]
            spread(signal, columns)
            kernel = turned(messages[k][PIX : PIX + ROWS, :])
            for row in range(0, PIX, MAIN):
                rows = slice(row, row + MAIN)
                back = backward_dot(columns, row, kernel)
                change[rows, :] = terms[k][rows, :].astype(F32) + (change[rows, :] + COARSE * back)
        leave[...] = change[...].astype(BF16)


def backward_chain(head, past, me, entry, slopes, terms, messages, held):
    count = len(messages)
    outs = [shape(IMAGE, BF16)]
    outs += [shape(IMAGE if count > 1 else (16, CH), BF16)] * count
    out = call(
        functools.partial(backward_kernel, count, head, past, len(held)),
        outs,
        [SMEM] + [VMEM] * (2 + 2 * count + len(held)),
        [PADDED, COLUMNS, pltpu.VMEM(IMAGE, F32)],
    )(me, entry, slopes, *terms, *messages, *held)
    return out[0], out[1:]


def picked(me, sources):
    for ref, takers in sources:
        hit = functools.reduce(jnp.logical_or, [me[0] == taker for taker in takers])
        yield hit, ref


SPOTS = [tuple(low + r for low in LOWS) for r in range(SEG)]
FORWARD_TAKERS = [(FIRST,), (LAST,), (END,)] + SPOTS
BACKWARD_TAKERS = [(0,), (FIRST,), (LAST,)] + SPOTS


def fine_kernel(me, start, adjoint, behind, kernels, biases, *refs):
    sources = refs[: len(FORWARD_TAKERS)]
    ends, states, slopes, term, state, columns, lam = refs[len(FORWARD_TAKERS) :]
    clear(state, columns)
    for hit, ref in picked(me, [(start, (0,))] + list(zip(sources, FORWARD_TAKERS))):

        @pl.when(hit)
        def _():
            state[8 : PIX + 8, :] = ref[...].astype(F32)

    def layer(n, _):
        spread(state, columns)
        states[n] = columns[SIDE : SIDE + PIX, CH : 2 * CH]
        kernel = kernels[n]
        bias = biases[n]
        for row in range(0, PIX, MAIN):
            at = slice(8 + row, 8 + row + MAIN)
            act = jnp.tanh(forward_dot(columns, row, kernel) + bias)
            slopes[n, row : row + MAIN, :] = (1.0 - act * act).astype(BF16)
            state[at, :] = state[at, :] + step_size * act
        return 0

    lax.fori_loop(0, DEPTH, layer, 0)
    ends[...] = state[8 : PIX + 8, :]
    lam[...] = adjoint[...]

    def back(i, _):
        n = DEPTH - 1 - i
        state[8 : PIX + 8, :] = slopes[n].astype(F32) * lam[...]
        spread(state, columns)
        kernel = turned(kernels.at[n])
        for row in range(0, PIX, MAIN):
            rows = slice(row, row + MAIN)
            lam[rows, :] = lam[rows, :] + step_size * backward_dot(columns, row, kernel)
        return 0

    lax.fori_loop(0, DEPTH, back, 0)
    term[...] = (lam[...] - behind[...].astype(F32)).astype(BF16)


def final_kernel(scale, me, adjoint, kernels, states, slopes, *refs):
    sources = refs[: len(BACKWARD_TAKERS)]
    lam, grads, signal, columns, sums = refs[len(BACKWARD_TAKERS) :]
    clear(signal, columns)
    sums[...] = jnp.zeros((8, CH), F32)
    lam[...] = adjoint[...]
    for hit, ref in picked(me, zip(sources, BACKWARD_TAKERS)):

        @pl.when(hit)
        def _():
            lam[...] = lam[...] + ref[...].astype(F32)

    def layer(i, _):
        n = DEPTH - 1 - i
        signal[8 : PIX + 8, :] = slopes[n].astype(F32) * lam[...]
        spread(signal, columns)
        centre = columns[SIDE : SIDE + PIX, CH : 2 * CH].astype(F32)
        sums[pl.ds(n, 1), :] = jnp.sum(centre, axis=0, keepdims=True) * scale
        kernel = turned(kernels.at[n])
        for row in range(0, PIX, MAIN):
            rows = slice(row, row + MAIN)
            lam[rows, :] = lam[rows, :] + step_size * backward_dot(columns, row, kernel)
        found = jnp.dot(states[n].T, windows(columns, 0, PIX), preferred_element_type=F32)
        for tap in range(TAPS):
            part = (found[:, (8 - tap) * CH : (9 - tap) * CH] * scale).astype(BF16)
            row = tap * CH
            while row < (tap + 1) * CH:
                piece, at = row // PIECE, row % PIECE
                size = min(PIECE - at, (tap + 1) * CH - row)
                grads[ROWS // PIECE * n + piece, at : at + size, :] = part[
                    row - tap * CH : row - tap * CH + size, :
                ]
                row += size
        return 0

    lax.fori_loop(0, DEPTH, layer, 0)
    tail = sums[...].astype(BF16)
    for peer in range(PEERS):
        grads[peer, PIECE : PIECE + 8, :] = tail


def add_kernel(parts, total, bias):
    acc = parts[0].astype(F32)
    for peer in range(1, PEERS):
        acc = acc + parts[peer].astype(F32)
    total[...] = acc[:PIECE, :].astype(BF16)
    bias[...] = acc[PIECE : PIECE + 8, :]


def move(x, pairs):
    return lax.ppermute(x, "layer", pairs)


def local(starts, weights, biases, adj_ends):
    me = lax.axis_index("layer").astype(jnp.int32).reshape(1)
    images = starts.shape[1] * lax.axis_size("dp")
    scale = 1.0 / (SIDE * math.sqrt(images))
    start = starts.reshape(IMAGE)
    adjoint = adj_ends.reshape(IMAGE)
    kernels = weights.reshape(DEPTH, ROWS, CH)
    rows = biases.astype(F32).reshape(DEPTH, 1, CH)
    behind = move(adjoint.astype(BF16), [(i, i + 1) for i in range(END)])

    short, message = call(
        relax_kernel,
        [shape(IMAGE, BF16), shape((MSG, CH), BF16)],
        [SMEM] + [VMEM] * 3,
        [PADDED, COLUMNS, pltpu.VMEM(IMAGE, F32)],
    )(me, start, kernels, rows)

    def to_head(x):
        return [
            x if r == SPOT else move(x, [(low + r, head) for low, head in zip(LOWS, HEADS)])
            for r in range(SEG)
        ]

    def from_head(marks):
        return [
            mark if r == SPOT else move(mark, [(head, low + r) for low, head in zip(LOWS, HEADS)])
            for r, mark in enumerate(marks)
        ]

    entry1 = move(short, [(0, FIRST)])
    messages = to_head(message)
    leave, first_held = forward_chain(FIRST, LAST, me, entry1, [message], ())
    entry = move(leave, [(FIRST, HEADS[0])])
    leave, held = forward_chain(HEADS[0], None, me, entry, messages, ())
    entry = move(leave, [(HEADS[0], HEADS[1])])
    leave, held = forward_chain(HEADS[1], HEADS[0], me, entry, messages, tuple(held))
    entry14 = move(leave, [(HEADS[1], LAST)])
    leave, first_held = forward_chain(LAST, FIRST, me, entry14, [message], tuple(first_held))
    entry15 = move(leave, [(LAST, END)])
    slopes, marks = held[0], held[1:]
    first_slopes = first_held[0]

    ends, states, fine_slopes, term = call(
        fine_kernel,
        [shape(IMAGE, F32), shape((DEPTH,) + IMAGE, BF16), shape((DEPTH,) + IMAGE, BF16), shape(IMAGE, BF16)],
        [SMEM] + [VMEM] * (5 + len(FORWARD_TAKERS)),
        [PADDED, COLUMNS, pltpu.VMEM(IMAGE, F32)],
    )(me, start, adjoint, behind, kernels, rows, entry1, entry14, entry15, *from_head(marks))

    back14 = move(term, [(END, LAST)])
    terms = to_head(term)
    leave, _ = backward_chain(LAST, None, me, back14, first_slopes, [term], [message], ())
    entry = move(leave, [(LAST, HEADS[1])])
    leave, marks = backward_chain(HEADS[1], None, me, entry, slopes, terms, messages, ())
    entry = move(leave, [(HEADS[1], HEADS[0])])
    leave, marks = backward_chain(HEADS[0], HEADS[1], me, entry, slopes, terms, messages, tuple(marks))
    back1 = move(leave, [(HEADS[0], FIRST)])
    leave, _ = backward_chain(FIRST, None, me, back1, first_slopes, [term], [message], ())
    back0 = move(leave, [(FIRST, 0)])

    lam, grads = call(
        functools.partial(final_kernel, scale),
        [shape(IMAGE, F32), shape((PEERS, PIECE + 8, CH), BF16)],
        [SMEM] + [VMEM] * (4 + len(BACKWARD_TAKERS)),
        [PADDED, COLUMNS, pltpu.VMEM((8, CH), F32)],
    )(me, adjoint, kernels, states, fine_slopes, back0, back1, back14, *from_head(marks))

    parts = lax.all_to_all(grads, "dp", 0, 0)
    total, bias_total = call(
        add_kernel, [shape((PIECE, CH), BF16), shape((8, CH), F32)], [VMEM], []
    )(parts)
    copies = jnp.broadcast_to(total[None], (PEERS, PIECE, CH))
    whole = lax.all_to_all(copies, "dp", 0, 0).astype(F32)
    return (
        ends.reshape(starts.shape),
        lam.reshape(starts.shape),
        whole.reshape(weights.shape),
        bias_total[:DEPTH],
    )


def solution(mesh):
    in_specs = (
        P("layer", "dp", None, None, None),
        P("layer", None, None, None),
        P("layer", None),
        P("layer", "dp", None, None, None),
    )
    out_specs = (
        P("layer", "dp", None, None, None),
        P("layer", "dp", None, None, None),
        P("layer", None, None, None),
        P("layer", None),
    )
    return jax.shard_map(local, mesh=mesh, in_specs=in_specs, out_specs=out_specs, check_vma=False)
```
